512 devices in a mesh: section: 16 (over z, core), seq: 32 (over y, x).
Axes of the slice: x: 4, y: 8, z: 8, core: 2. Of those that a mesh axis runs over, the one named last changes fastest.
Arguments:
- query: bfloat16 [16384, 4096], P('seq', 'section'), may hold values from -6 to 6
- key_proj: bfloat16 [16384, 4096], P('seq', 'section'), may hold values from -6 to 6
- value_proj: bfloat16 [16384, 4096], P('seq', 'section'), may hold values from -6 to 6
- filter_taps: float32 [16384, 4096], P('seq', 'section'), may hold values from -2 to 2
- skip_gain: float32 [4096], P('section'), may hold values from -4 to 4
Outputs:
- handed_on: bfloat16 [16384, 4096], P('seq', 'section')
The draws below stay inside these ranges and needn't reach their ends.
All inputs are finite; a program needn't handle non-finite values.
Results may differ from the reference program's by a relative error of at most 0.00155.
Values may be sent and summed in bfloat16 or wider, within the bound.
No kernel may reach another device: no remote copies, remote signals or barrier semaphores. Data moves between devices by JAX's collectives and lax.ppermute only.
A program may use at most 64 MiB of HBM per device.

```python
import math
import jax
import jax.numpy as jnp
from jax import lax

CH_DEV = 256
TOKENS = 16384
CH = 4096


def draw_filter_taps(key, part):
    keys = jax.random.split(jax.random.fold_in(key, 17), 6)
    slow = jax.random.bernoulli(keys[0], 0.5, (CH,))
    noise = jnp.clip(jax.random.normal(keys[3], (TOKENS, CH), jnp.float32), -5.0, 5.0)
    floor_noise = jnp.clip(jax.random.normal(keys[5], (TOKENS, CH), jnp.float32), -5.0, 5.0)
    long_tau = jnp.exp(jax.random.uniform(keys[1], (CH,), jnp.float32, math.log(TOKENS / 2.0), math.log(4.0 * TOKENS)))
    short_tau = jnp.exp(jax.random.uniform(keys[2], (CH,), jnp.float32, math.log(16.0), math.log(TOKENS / 2.0)))
    floor_tau = jnp.exp(jax.random.uniform(keys[4], (CH,), jnp.float32, math.log(1.0 * TOKENS), math.log(4.0 * TOKENS)))
    decay_len = jnp.where(slow, long_tau, short_tau)
    lags = jnp.arange(TOKENS, dtype=jnp.float32)[:, None]
    envelope = jnp.exp(-lags / decay_len[None, :]) * jnp.sqrt(1.0 - jnp.exp(-2.0 / decay_len[None, :]))
    floor_env = 0.15 * jnp.exp(-lags / floor_tau[None, :]) * jnp.sqrt(1.0 - jnp.exp(-2.0 / floor_tau[None, :]))
    return (envelope * noise + floor_env * floor_noise).astype(jnp.float32)


def levels(rng, shape, cuts, least, top_value):
    gain, own = 1.0, jax.random.fold_in(rng, 6)
    for axis_at, blocks in cuts:
        steps = jnp.exp(jax.random.uniform(jax.random.fold_in(own, axis_at), (blocks,), jnp.float32, least / len(cuts), top_value / len(cuts)))
        gain = gain * jnp.repeat(steps, shape[axis_at] // blocks).reshape([-1 if axis == axis_at else 1 for axis in range(len(shape))])
    return gain


def centred(stream_key, shape, width, most, shards=(), kind=jnp.bfloat16):
    level = levels(stream_key, shape, shards, -0.22, 0.18) if shards else 1.0
    entries = jax.random.normal(stream_key, shape, jnp.float32) * width * level
    return jnp.minimum(jnp.maximum(entries, -most), most).astype(kind)


def setup_inputs(seed: int = 0) -> dict:
    seeds = jax.random.split(jax.random.key(seed), 6)
    return {
        "query": centred(seeds[0], (TOKENS, CH), 1.0, 6.0, ((0, 32), (1, 16))),
        "key_proj": centred(seeds[1], (TOKENS, CH), 1.0, 6.0, ((0, 32), (1, 16))),
        "value_proj": centred(seeds[2], (TOKENS, CH), 1.0, 6.0, ((0, 32), (1, 16))),
        "filter_taps": draw_filter_taps(jax.random.fold_in(seeds[5], 71), 0),
        "skip_gain": centred(seeds[4], (CH,), 1.0, 4.0, ((0, 16),), jnp.float32),
    }


def convolve_block(pair):
    signal, taps = pair
    total = 2 * TOKENS
    spectrum = jnp.fft.rfft(signal, n=total, axis=0) * jnp.fft.rfft(taps, n=total, axis=0)
    return jnp.fft.irfft(spectrum, n=total, axis=0)[:TOKENS].astype(jnp.float32)


def reference(query, key_proj, value_proj, filter_taps, skip_gain):
    driven = key_proj.astype(jnp.float32) * value_proj.astype(jnp.float32)
    blocks = CH // CH_DEV
    signal = driven.reshape(TOKENS, blocks, CH_DEV).transpose(1, 0, 2)
    taps = filter_taps.reshape(TOKENS, blocks, CH_DEV).transpose(1, 0, 2)
    conv = lax.map(convolve_block, (signal, taps)).transpose(1, 0, 2).reshape(TOKENS, CH)
    mixed = (query.astype(jnp.float32) * (conv + skip_gain[None, :] * driven)).astype(jnp.bfloat16)
    return jnp.roll(mixed, CH_DEV, axis=1)
```

```python
import jax
import jax.numpy as jnp
import numpy as np
from jax import lax
from jax.experimental import pallas as pl
from jax.experimental.pallas import tpu as pltpu
from jax.sharding import PartitionSpec as P

F16_TOP = 14.0
SCALE_LANES = 128


def passed_along(value, axis, by):
    length = lax.axis_size(axis)
    return lax.ppermute(value, axis, [(i, (i + by) % length) for i in range(length)])


def regrouped(blocks):
    return lax.all_to_all(blocks, "seq", split_axis=0, concat_axis=0, tiled=True)


def split_bf16(table):
    high = table.astype(jnp.bfloat16)
    return high, (table - high.astype(np.float64)).astype(jnp.bfloat16)


def tables(shards, group, tok_rows):
    total = shards * tok_rows
    lanes = 128
    tiles = tok_rows // lanes
    s = np.arange(shards)
    k = np.arange(shards) + 0.25
    own = np.eye(group)
    phase = 2.0 * np.pi * np.outer(k, s) / shards
    cosine, sine = np.kron(np.cos(phase), own), np.kron(np.sin(phase), own)
    fwd_rows = np.concatenate([cosine, -sine], axis=0)
    inv_rows = np.concatenate([cosine.T, -sine.T], axis=1) / total
    b = np.arange(lanes)
    turn = 2.0 * np.pi * np.outer(b, b) / lanes
    c, n = np.cos(turn), np.sin(turn)
    fwd_lanes = np.block([[c, -n], [n, c]])
    inv_lanes = np.block([[c, n], [-n, c]])
    near = np.repeat(2.0 * np.pi * np.outer(k, np.arange(tiles)) / (shards * tiles), lanes, axis=1)
    freq = k[:, None] + shards * np.repeat(np.arange(tiles), lanes)[None, :]
    far = 2.0 * np.pi * freq * np.tile(b, tiles)[None, :] / total
    twiddles = np.stack([np.cos(near), np.sin(near), np.cos(far), np.sin(far)])[:, :, None, :].astype(np.float32)
    rows_high, rows_low = split_bf16(fwd_rows)
    back_high, back_low = split_bf16(inv_rows)
    lane_high, lane_low = split_bf16(fwd_lanes)
    home_high, home_low = split_bf16(inv_lanes)
    return (
        np.concatenate([rows_high, rows_low], axis=1),
        np.concatenate([back_high, back_low], axis=1),
        np.concatenate([lane_high, lane_low], axis=0),
        np.concatenate([home_high, home_low], axis=0),
        twiddles,
    )


def halves(value):
    high = value.astype(jnp.bfloat16)
    low = (value - high.astype(jnp.float32)).astype(jnp.bfloat16)
    return high, low


def left_product(table_ref, value):
    high, low = halves(value)
    depth = value.shape[0]
    table = jnp.concatenate([table_ref[:, :depth], table_ref[:, :depth], table_ref[:, depth:]], axis=1)
    return jnp.dot(table, jnp.concatenate([high, low, high], axis=0), preferred_element_type=jnp.float32)


def right_product(value, table_ref):
    high, low = halves(value)
    depth = value.shape[1]
    table = jnp.concatenate([table_ref[:depth], table_ref[:depth], table_ref[depth:]], axis=0)
    return jnp.dot(jnp.concatenate([high, low, high], axis=1), table, preferred_element_type=jnp.float32)


def tile_of(value, index):
    return value[:, index * 128 : (index + 1) * 128]


def turned(real, imag, cosine, sine):
    return real * cosine - imag * sine, real * sine + imag * cosine


def four_point(r, q, sign):
    r02, q02, r13, q13 = r[0] + r[2], q[0] + q[2], r[1] + r[3], q[1] + q[3]
    d02, e02, d13, e13 = r[0] - r[2], q[0] - q[2], r[1] - r[3], q[1] - q[3]
    reals = [r02 + r13, d02 - sign * e13, r02 - r13, d02 + sign * e13]
    imags = [q02 + q13, e02 + sign * d13, q02 - q13, e02 - sign * d13]
    return reals, imags


def phase(tw_ref, part, tile, group):
    rows = tw_ref[part, :, :, tile * 128 : (tile + 1) * 128]
    count = rows.shape[0]
    return jnp.broadcast_to(rows, (count, group, 128)).reshape(count * group, 128)


def spectrum(value, rows_ref, lanes_ref, tw_ref):
    half = value.shape[0]
    group = half // tw_ref.shape[1]
    both = left_product(rows_ref, value)
    reals, imags = [tile_of(both[:half], 0)], [tile_of(both[half:], 0)]
    for j in range(1, 4):
        real, imag = turned(
            tile_of(both[:half], j),
            tile_of(both[half:], j),
            phase(tw_ref, 0, j, group),
            -phase(tw_ref, 1, j, group),
        )
        reals.append(real)
        imags.append(imag)
    reals, imags = four_point(reals, imags, -1.0)
    out = []
    for m in range(4):
        real, imag = turned(reals[m], imags[m], phase(tw_ref, 2, m, group), -phase(tw_ref, 3, m, group))
        out.append(right_product(jnp.concatenate([real, imag], axis=1), lanes_ref))
    return out


def wire_scale(rows):
    top = jnp.maximum(jnp.max(jnp.abs(rows), axis=1, keepdims=True), 1e-30)
    return F16_TOP - jnp.ceil(jnp.log2(top))


def as_lanes(column):
    return jnp.broadcast_to(column, (column.shape[0], SCALE_LANES))


def pack_kernel(key_hbm, value_hbm, taps_hbm, out_ref, key_ref, value_ref, taps_ref, sems):
    copies = [
        pltpu.make_async_copy(source, target, sems.at[i])
        for i, (source, target) in enumerate(
            [(key_hbm, key_ref), (value_hbm, value_ref), (taps_hbm, taps_ref)]
        )
    ]
    for copy in copies:
        copy.start()
    for copy in copies:
        copy.wait()
    span = key_ref.shape[0]
    driven = key_ref[...].astype(jnp.float32) * value_ref[...].astype(jnp.float32)
    sig, tap = driven.T, taps_ref[...].T
    sig_exp, tap_exp = wire_scale(sig), wire_scale(tap)
    out_ref[:, :span] = sig * jnp.exp2(sig_exp)
    out_ref[:, span : 2 * span] = tap * jnp.exp2(tap_exp)
    lane = lax.broadcasted_iota(jnp.int32, (sig.shape[0], SCALE_LANES), 1)
    out_ref[:, 2 * span :] = jnp.where(lane == 0, as_lanes(sig_exp), as_lanes(tap_exp))


def convolve_kernel(in_ref, rows_ref, back_ref, lanes_ref, home_ref, tw_ref, out_ref):
    span = tw_ref.shape[3]
    sig_in = in_ref[:, :span] * jnp.exp2(-in_ref[:, 2 * span : 2 * span + 1])
    tap_in = in_ref[:, span : 2 * span] * jnp.exp2(-in_ref[:, 2 * span + 1 : 2 * span + 2])
    sig = spectrum(sig_in, rows_ref, lanes_ref, tw_ref)
    tap = spectrum(tap_in, rows_ref, lanes_ref, tw_ref)
    group = in_ref.shape[0] // tw_ref.shape[1]
    reals, imags = [], []
    for m in range(4):
        real, imag = turned(sig[m][:, :128], sig[m][:, 128:], tap[m][:, :128], tap[m][:, 128:])
        back = right_product(jnp.concatenate([real, imag], axis=1), home_ref)
        real, imag = turned(back[:, :128], back[:, 128:], phase(tw_ref, 2, m, group), phase(tw_ref, 3, m, group))
        reals.append(real)
        imags.append(imag)
    reals, imags = four_point(reals, imags, 1.0)
    for j in range(1, 4):
        reals[j], imags[j] = turned(reals[j], imags[j], phase(tw_ref, 0, j, group), phase(tw_ref, 1, j, group))
    real, imag = jnp.concatenate(reals, axis=1), jnp.concatenate(imags, axis=1)
    conv = left_product(back_ref, jnp.concatenate([real, imag], axis=0))
    conv_exp = wire_scale(conv)
    out_ref[:, :span] = conv * jnp.exp2(conv_exp)
    out_ref[:, span:] = as_lanes(conv_exp)


def mix_kernel(conv_ref, query_ref, key_ref, value_ref, gain_ref, out_ref):
    span = query_ref.shape[0]
    conv = (conv_ref[:, :span] * jnp.exp2(-conv_ref[:, span : span + 1])).T
    driven = key_ref[...].astype(jnp.float32) * value_ref[...].astype(jnp.float32)
    mixed = query_ref[...].astype(jnp.float32) * (conv + gain_ref[...] * driven)
    out_ref[...] = mixed.astype(jnp.bfloat16)


def call(kernel, shape, dtype, name, vmem_mib, **more):
    return pl.pallas_call(
        kernel,
        out_shape=jax.ShapeDtypeStruct(shape, dtype),
        compiler_params=pltpu.CompilerParams(vmem_limit_bytes=vmem_mib * 2**20),
        name=name,
        **more,
    )


def on_wire(rows, shards):
    wide = rows.astype(jnp.float16).reshape(shards, rows.shape[0] // shards, rows.shape[1])
    return regrouped(wide).reshape(rows.shape).astype(jnp.float32)


def on_device(query, key_proj, value_proj, filter_taps, skip_gain):
    span, width = query.shape
    shards = lax.axis_size("seq")
    group = width // shards
    packed = call(
        pack_kernel,
        (width, 2 * span + SCALE_LANES),
        jnp.float32,
        "pack",
        12,
        in_specs=[pl.BlockSpec(memory_space=pltpu.HBM)] * 3,
        scratch_shapes=[
            pltpu.VMEM((span, width), jnp.bfloat16),
            pltpu.VMEM((span, width), jnp.bfloat16),
            pltpu.VMEM((span, width), jnp.float32),
            pltpu.SemaphoreType.DMA((3,)),
        ],
    )(*[pltpu.with_memory_space_constraint(a, pltpu.HBM) for a in (key_proj, value_proj, filter_taps)])
    conv = call(convolve_kernel, (width, span + SCALE_LANES), jnp.float32, "convolve", 28)(
        on_wire(packed, shards), *tables(shards, group, span)
    )
    mixed = call(mix_kernel, (span, width), jnp.bfloat16, "mix", 12)(
        on_wire(conv, shards), query, key_proj, value_proj, skip_gain[None, :]
    )
    return passed_along(mixed, "section", 1)


def solution(mesh):
    placed = (
        P("seq", "section"),
        P("seq", "section"),
        P("seq", "section"),
        P("seq", "section"),
        P("section"),
    )
    return jax.shard_map(
        on_device, mesh=mesh, in_specs=placed, out_specs=P("seq", "section"), check_vma=False
    )
```

```python
import jax
import jax.numpy as jnp
import numpy as np
from jax import lax
from jax.experimental import pallas as pl
from jax.experimental.pallas import tpu as pltpu
from jax.sharding import PartitionSpec as P

F16_TOP = 14.0
SCALE_LANES = 128
FOLD = 4


def passed_along(value, axis, by):
    length = lax.axis_size(axis)
    return lax.ppermute(value, axis, [(i, (i + by) % length) for i in range(length)])


def regrouped(blocks):
    return lax.all_to_all(blocks, "seq", split_axis=0, concat_axis=0, tiled=True)


def split_bf16(table):
    high = table.astype(jnp.bfloat16)
    return high, (table - high.astype(np.float64)).astype(jnp.bfloat16)


def tables(shards, group, tok_rows):
    total = shards * tok_rows
    lanes = 128
    tiles = tok_rows // lanes
    s = np.arange(shards)
    k = np.arange(shards) + 0.25
    own = np.eye(group)
    phase = 2.0 * np.pi * np.outer(k, s) / shards
    cosine, sine = np.kron(np.cos(phase), own), np.kron(np.sin(phase), own)
    fwd_rows = np.concatenate([cosine, -sine], axis=0)
    inv_rows = np.concatenate([cosine.T, -sine.T], axis=1) / total
    b = np.arange(lanes)
    turn = 2.0 * np.pi * np.outer(b, b) / lanes
    c, n = np.cos(turn), np.sin(turn)
    fwd_lanes = np.block([[c, -n], [n, c]])
    inv_lanes = np.block([[c, n], [-n, c]])
    near = np.repeat(2.0 * np.pi * np.outer(k, np.arange(tiles)) / (shards * tiles), lanes, axis=1)
    freq = k[:, None] + shards * np.repeat(np.arange(tiles), lanes)[None, :]
    far = 2.0 * np.pi * freq * np.tile(b, tiles)[None, :] / total
    twiddles = np.stack([np.cos(near), np.sin(near), np.cos(far), np.sin(far)])[:, :, None, :].astype(np.float32)
    rows_high, rows_low = split_bf16(fwd_rows)
    back_high, back_low = split_bf16(inv_rows)
    lane_high, lane_low = split_bf16(fwd_lanes)
    home_high, home_low = split_bf16(inv_lanes)
    return (
        np.concatenate([rows_high, rows_low], axis=1),
        np.concatenate([back_high, back_low], axis=1),
        np.concatenate([lane_high, lane_low], axis=0),
        np.concatenate([home_high, home_low], axis=0),
        twiddles,
    )


def halves(value):
    high = value.astype(jnp.bfloat16)
    low = (value - high.astype(jnp.float32)).astype(jnp.bfloat16)
    return high, low


def left_product(table_ref, value):
    high, low = halves(value)
    depth = value.shape[0]
    table = jnp.concatenate([table_ref[:, :depth], table_ref[:, :depth], table_ref[:, depth:]], axis=1)
    return jnp.dot(table, jnp.concatenate([high, low, high], axis=0), preferred_element_type=jnp.float32)


def right_product(value, table_ref):
    high, low = halves(value)
    depth = value.shape[1]
    table = jnp.concatenate([table_ref[:depth], table_ref[:depth], table_ref[depth:]], axis=0)
    return jnp.dot(jnp.concatenate([high, low, high], axis=1), table, preferred_element_type=jnp.float32)


def tile_of(value, index):
    return value[:, index * 128 : (index + 1) * 128]


def turned(real, imag, cosine, sine):
    return real * cosine - imag * sine, real * sine + imag * cosine


def four_point(r, q, sign):
    r02, q02, r13, q13 = r[0] + r[2], q[0] + q[2], r[1] + r[3], q[1] + q[3]
    d02, e02, d13, e13 = r[0] - r[2], q[0] - q[2], r[1] - r[3], q[1] - q[3]
    reals = [r02 + r13, d02 - sign * e13, r02 - r13, d02 + sign * e13]
    imags = [q02 + q13, e02 + sign * d13, q02 - q13, e02 - sign * d13]
    return reals, imags


def phase(tw_ref, part, tile, group):
    rows = tw_ref[part, :, :, tile * 128 : (tile + 1) * 128]
    count = rows.shape[0]
    return jnp.broadcast_to(rows, (count, group, 128)).reshape(count * group, 128)


def spectrum(value, rows_ref, lanes_ref, tw_ref):
    half = value.shape[0]
    group = half // tw_ref.shape[1]
    both = left_product(rows_ref, value)
    reals, imags = [tile_of(both[:half], 0)], [tile_of(both[half:], 0)]
    for j in range(1, 4):
        real, imag = turned(
            tile_of(both[:half], j),
            tile_of(both[half:], j),
            phase(tw_ref, 0, j, group),
            -phase(tw_ref, 1, j, group),
        )
        reals.append(real)
        imags.append(imag)
    reals, imags = four_point(reals, imags, -1.0)
    out = []
    for m in range(4):
        real, imag = turned(reals[m], imags[m], phase(tw_ref, 2, m, group), -phase(tw_ref, 3, m, group))
        out.append(right_product(jnp.concatenate([real, imag], axis=1), lanes_ref))
    return out


def wire_scale(rows):
    top = jnp.maximum(jnp.max(jnp.abs(rows), axis=1, keepdims=True), 1e-30)
    return F16_TOP - jnp.ceil(jnp.log2(top))


def store_folded(out_ref, fold_ref, parts):
    rows = out_ref.shape[0]
    span = parts[0].shape[1]
    lane = lax.broadcasted_iota(jnp.int32, (rows, SCALE_LANES), 1)
    tail = jnp.zeros((rows, SCALE_LANES), jnp.float32)
    for n, part in enumerate(parts):
        exponent = wire_scale(part)
        scaled = part * jnp.exp2(exponent)
        tiles = span // 128
        for tile in range(tiles):
            fold_ref[tile] = tile_of(scaled, tile)
        fold_ref[tiles] = jnp.broadcast_to(exponent, (part.shape[0], SCALE_LANES))
        for i in range(FOLD):
            at = (i * len(parts) + n) * span
            for tile in range(tiles):
                out_ref[:, at + tile * 128 : at + tile * 128 + 128] = fold_ref[tile, pl.ds(i, rows, stride=FOLD), :]
            own = fold_ref[tiles, pl.ds(i, rows, stride=FOLD), :]
            tail = jnp.where(lane == i * len(parts) + n, own, tail)
    out_ref[:, FOLD * len(parts) * span :] = tail


def load_folded(in_ref, fold_ref, count, n):
    rows, tiles = in_ref.shape[0], fold_ref.shape[0]
    for i in range(FOLD):
        lane = FOLD * count * tiles * 128 + i * count + n
        scale = jnp.exp2(-in_ref[:, lane : lane + 1])
        for tile in range(tiles):
            at = ((i * count + n) * tiles + tile) * 128
            fold_ref[tile, pl.ds(i, rows, stride=FOLD), :] = in_ref[:, at : at + 128] * scale
    return jnp.concatenate([fold_ref[tile] for tile in range(tiles)], axis=1)


def pack_kernel(*refs):
    count = (len(refs) - 8) // 2
    sources, outs = refs[: 3 + count], refs[3 + count : 4 + 2 * count]
    key_ref, value_ref, taps_ref, fold_ref, sems = refs[4 + 2 * count :]
    targets = (key_ref, value_ref, taps_ref) + outs[1:]
    copies = [pltpu.make_async_copy(a, b, sems.at[n]) for n, (a, b) in enumerate(zip(sources, targets))]
    for copy in copies[:3]:
        copy.start()
    copies[0].wait()
    copies[1].wait()
    driven = key_ref[...].astype(jnp.float32) * value_ref[...].astype(jnp.float32)
    copies[2].wait()
    for copy in copies[3:]:
        copy.start()
    store_folded(outs[0], fold_ref, [driven.T, taps_ref[...].T])
    for copy in copies[3:]:
        copy.wait()


def convolve_kernel(in_ref, rows_ref, back_ref, lanes_ref, home_ref, tw_ref, out_ref, sig_ref, tap_ref, fold_ref):
    sig_in = load_folded(in_ref, sig_ref, 2, 0)
    tap_in = load_folded(in_ref, tap_ref, 2, 1)
    sig = spectrum(sig_in, rows_ref, lanes_ref, tw_ref)
    tap = spectrum(tap_in, rows_ref, lanes_ref, tw_ref)
    group = sig_ref.shape[1] // tw_ref.shape[1]
    reals, imags = [], []
    for m in range(4):
        real, imag = turned(sig[m][:, :128], sig[m][:, 128:], tap[m][:, :128], tap[m][:, 128:])
        back = right_product(jnp.concatenate([real, imag], axis=1), home_ref)
        real, imag = turned(back[:, :128], back[:, 128:], phase(tw_ref, 2, m, group), phase(tw_ref, 3, m, group))
        reals.append(real)
        imags.append(imag)
    reals, imags = four_point(reals, imags, 1.0)
    for j in range(1, 4):
        reals[j], imags[j] = turned(reals[j], imags[j], phase(tw_ref, 0, j, group), phase(tw_ref, 1, j, group))
    real, imag = jnp.concatenate(reals, axis=1), jnp.concatenate(imags, axis=1)
    conv = left_product(back_ref, jnp.concatenate([real, imag], axis=0))
    store_folded(out_ref, fold_ref, [conv])


def mix_kernel(conv_ref, query_ref, key_ref, value_ref, gain_ref, out_ref, fold_ref):
    conv = load_folded(conv_ref, fold_ref, 1, 0).T
    driven = key_ref[...].astype(jnp.float32) * value_ref[...].astype(jnp.float32)
    mixed = query_ref[...].astype(jnp.float32) * (conv + gain_ref[...] * driven)
    out_ref[...] = mixed.astype(jnp.bfloat16)


def call(kernel, shape, dtype, name, vmem_mib, **more):
    return pl.pallas_call(
        kernel,
        out_shape=jax.ShapeDtypeStruct(shape, dtype),
        compiler_params=pltpu.CompilerParams(vmem_limit_bytes=vmem_mib * 2**20),
        name=name,
        **more,
    )


def on_wire(rows, shards):
    wide = rows.astype(jnp.float16).reshape(shards, rows.shape[0] // shards, rows.shape[1])
    return lax.optimization_barrier(regrouped(wide).reshape(rows.shape)).astype(jnp.float32)


def on_device(query, key_proj, value_proj, filter_taps, skip_gain):
    span, width = query.shape
    shards = lax.axis_size("seq")
    group = width // shards
    rows = width // FOLD
    folded = pltpu.VMEM((span // 128 + 1, width, 128), jnp.float32)
    unfolded = pltpu.VMEM((span // 128, width, 128), jnp.float32)
    phases = tables(shards, group, span)
    sources = [
        pltpu.with_memory_space_constraint(jnp.asarray(a), pltpu.HBM)
        for a in (key_proj, value_proj, filter_taps) + phases
    ]
    wire = jax.ShapeDtypeStruct((rows, 2 * FOLD * span + SCALE_LANES), jnp.float32)
    packed, *phases = pl.pallas_call(
        pack_kernel,
        out_shape=[wire] + [jax.ShapeDtypeStruct(a.shape, a.dtype) for a in phases],
        in_specs=[pl.BlockSpec(memory_space=pltpu.HBM)] * len(sources),
        out_specs=[pl.BlockSpec(memory_space=pltpu.VMEM)] * (1 + len(phases)),
        scratch_shapes=[
            pltpu.VMEM((span, width), jnp.bfloat16),
            pltpu.VMEM((span, width), jnp.bfloat16),
            pltpu.VMEM((span, width), jnp.float32),
            folded,
            pltpu.SemaphoreType.DMA((len(sources),)),
        ],
        compiler_params=pltpu.CompilerParams(vmem_limit_bytes=16 * 2**20),
        name="pack",
    )(*sources)
    conv = call(
        convolve_kernel,
        (rows, FOLD * span + SCALE_LANES),
        jnp.float32,
        "convolve",
        28,
        scratch_shapes=[unfolded, unfolded, folded],
    )(on_wire(packed, shards), *phases)
    mixed = call(mix_kernel, (span, width), jnp.bfloat16, "mix", 12, scratch_shapes=[unfolded])(
        on_wire(conv, shards), query, key_proj, value_proj, skip_gain[None, :]
    )
    return passed_along(mixed, "section", 1)


def solution(mesh):
    placed = (
        P("seq", "section"),
        P("seq", "section"),
        P("seq", "section"),
        P("seq", "section"),
        P("section"),
    )
    return jax.shard_map(
        on_device, mesh=mesh, in_specs=placed, out_specs=P("seq", "section"), check_vma=False
    )
```

```python
import jax
import jax.numpy as jnp
import numpy as np
from jax import lax
from jax.experimental import pallas as pl
from jax.experimental.pallas import tpu as pltpu
from jax.sharding import PartitionSpec as P

F16_TOP = 14.0
SCALE_LANES = 128
FOLD = 4
LAG_NANOS = 3300


def passed_along(value, axis, by):
    length = lax.axis_size(axis)
    return lax.ppermute(value, axis, [(i, (i + by) % length) for i in range(length)])


def regrouped(blocks):
    return lax.all_to_all(blocks, "seq", split_axis=0, concat_axis=0, tiled=True)


def split_bf16(table):
    high = table.astype(jnp.bfloat16)
    return high, (table - high.astype(np.float64)).astype(jnp.bfloat16)


def tables(shards, group, tok_rows):
    total = shards * tok_rows
    lanes = 128
    tiles = tok_rows // lanes
    s = np.arange(shards)
    k = np.arange(shards) + 0.25
    own = np.eye(group // FOLD)
    turn = 2.0 * np.pi * np.outer(k, s) / shards
    cosine, sine = np.kron(np.cos(turn), own), np.kron(np.sin(turn), own)
    fwd_rows = np.concatenate([cosine, -sine], axis=0)
    inv_rows = np.concatenate([cosine.T, -sine.T], axis=1) / total
    b = np.arange(lanes)
    turn = 2.0 * np.pi * np.outer(b, b) / lanes
    c, n = np.cos(turn), np.sin(turn)
    fwd_lanes = np.block([[c, -n], [n, c]])
    inv_lanes = np.block([[c, n], [-n, c]])
    near = np.repeat(2.0 * np.pi * np.outer(k, np.arange(tiles)) / (shards * tiles), lanes, axis=1)
    freq = k[:, None] + shards * np.repeat(np.arange(tiles), lanes)[None, :]
    far = 2.0 * np.pi * freq * np.tile(b, tiles)[None, :] / total
    twiddles = np.repeat(np.stack([np.cos(near), np.sin(near), np.cos(far), np.sin(far)]), group // FOLD, axis=1)
    rows_high, rows_low = split_bf16(fwd_rows)
    back_high, back_low = split_bf16(inv_rows)
    lane_high, lane_low = split_bf16(fwd_lanes)
    home_high, home_low = split_bf16(inv_lanes)
    return (
        np.concatenate([rows_high, rows_high, rows_low], axis=1),
        np.concatenate([back_high, back_high, back_low], axis=1),
        np.concatenate([lane_high, lane_low], axis=0),
        np.concatenate([home_high, home_low], axis=0),
        twiddles.astype(np.float32),
    )


def halves(value):
    high = value.astype(jnp.bfloat16)
    low = (value - high.astype(jnp.float32)).astype(jnp.bfloat16)
    return high, low


def left_product(table_ref, value):
    high, low = halves(value)
    return jnp.dot(table_ref[...], jnp.concatenate([high, low, high], axis=0), preferred_element_type=jnp.float32)


def right_product(value, table_ref):
    high, low = halves(value)
    depth = value.shape[1]
    table = jnp.concatenate([table_ref[:depth], table_ref[:depth], table_ref[depth:]], axis=0)
    return jnp.dot(jnp.concatenate([high, low, high], axis=1), table, preferred_element_type=jnp.float32)


def tile_of(value, index):
    return value[:, index * 128 : (index + 1) * 128]


def turned(real, imag, cosine, sine):
    return real * cosine - imag * sine, real * sine + imag * cosine


def four_point(r, q, sign):
    r02, q02, r13, q13 = r[0] + r[2], q[0] + q[2], r[1] + r[3], q[1] + q[3]
    d02, e02, d13, e13 = r[0] - r[2], q[0] - q[2], r[1] - r[3], q[1] - q[3]
    reals = [r02 + r13, d02 - sign * e13, r02 - r13, d02 + sign * e13]
    imags = [q02 + q13, e02 + sign * d13, q02 - q13, e02 - sign * d13]
    return reals, imags


def phase(tw_ref, part, tile):
    return jnp.concatenate([tw_ref[part, :, tile * 128 : (tile + 1) * 128]] * FOLD, axis=0)


def spectrum(blocks, rows_ref, lanes_ref, tw_ref):
    half = blocks[0].shape[0]
    outs = [left_product(rows_ref, block) for block in blocks]
    reals = [jnp.concatenate([tile_of(out[:half], j) for out in outs], axis=0) for j in range(4)]
    imags = [jnp.concatenate([tile_of(out[half:], j) for out in outs], axis=0) for j in range(4)]
    for j in range(1, 4):
        reals[j], imags[j] = turned(reals[j], imags[j], phase(tw_ref, 0, j), -phase(tw_ref, 1, j))
    reals, imags = four_point(reals, imags, -1.0)
    out = []
    for m in range(4):
        real, imag = turned(reals[m], imags[m], phase(tw_ref, 2, m), -phase(tw_ref, 3, m))
        out.append(right_product(jnp.concatenate([real, imag], axis=1), lanes_ref))
    return out


def wire_scale(rows):
    top = jnp.maximum(jnp.max(jnp.abs(rows), axis=1, keepdims=True), 1e-30)
    return F16_TOP - jnp.ceil(jnp.log2(top))


def store_folded(out_ref, fold_ref, parts):
    rows = out_ref.shape[0]
    span = parts[0].shape[1]
    lane = lax.broadcasted_iota(jnp.int32, (rows, SCALE_LANES), 1)
    tail = jnp.zeros((rows, SCALE_LANES), jnp.float32)
    for n, part in enumerate(parts):
        exponent = wire_scale(part)
        scaled = part * jnp.exp2(exponent)
        tiles = span // 128
        for tile in range(tiles):
            fold_ref[tile] = tile_of(scaled, tile)
        fold_ref[tiles] = jnp.broadcast_to(exponent, (part.shape[0], SCALE_LANES))
        for i in range(FOLD):
            at = (i * len(parts) + n) * span
            for tile in range(tiles):
                out_ref[:, at + tile * 128 : at + tile * 128 + 128] = fold_ref[tile, pl.ds(i, rows, stride=FOLD), :]
            own = fold_ref[tiles, pl.ds(i, rows, stride=FOLD), :]
            tail = jnp.where(lane == i * len(parts) + n, own, tail)
    out_ref[:, FOLD * len(parts) * span :] = tail


def load_folded(in_ref, fold_ref, count, n):
    rows, tiles = in_ref.shape[0], fold_ref.shape[0]
    for i in range(FOLD):
        lane = FOLD * count * tiles * 128 + i * count + n
        scale = jnp.exp2(-in_ref[:, lane : lane + 1])
        for tile in range(tiles):
            at = ((i * count + n) * tiles + tile) * 128
            fold_ref[tile, pl.ds(i, rows, stride=FOLD), :] = in_ref[:, at : at + 128] * scale
    return jnp.concatenate([fold_ref[tile] for tile in range(tiles)], axis=1)


def pack_kernel(*refs):
    count = (len(refs) - 8) // 2
    sources, outs = refs[: 3 + count], refs[3 + count : 4 + 2 * count]
    key_ref, value_ref, taps_ref, fold_ref, sems = refs[4 + 2 * count :]
    targets = (key_ref, value_ref, taps_ref) + outs[1:]
    copies = [pltpu.make_async_copy(a, b, sems.at[n]) for n, (a, b) in enumerate(zip(sources, targets))]
    for copy in copies:
        copy.start()
    copies[0].wait()
    copies[1].wait()
    driven = key_ref[...].astype(jnp.float32) * value_ref[...].astype(jnp.float32)
    copies[2].wait()

    @pl.when(lax.axis_index("section") % 2 == 0)
    def _():
        pl.delay(LAG_NANOS)

    store_folded(outs[0], fold_ref, [driven.T, taps_ref[...].T])
    for copy in copies[3:]:
        copy.wait()


def convolve_kernel(in_ref, rows_ref, back_ref, lanes_ref, home_ref, tw_ref, out_ref):
    rows, span = in_ref.shape[0], tw_ref.shape[2]

    def part(n):
        blocks = []
        for i in range(FOLD):
            at, lane = (2 * i + n) * span, 2 * FOLD * span + 2 * i + n
            blocks.append(in_ref[:, at : at + span] * jnp.exp2(-in_ref[:, lane : lane + 1]))
        return blocks

    sig = spectrum(part(0), rows_ref, lanes_ref, tw_ref)
    tap = spectrum(part(1), rows_ref, lanes_ref, tw_ref)
    reals, imags = [], []
    for m in range(4):
        real, imag = turned(sig[m][:, :128], sig[m][:, 128:], tap[m][:, :128], tap[m][:, 128:])
        back = right_product(jnp.concatenate([real, imag], axis=1), home_ref)
        real, imag = turned(back[:, :128], back[:, 128:], phase(tw_ref, 2, m), phase(tw_ref, 3, m))
        reals.append(real)
        imags.append(imag)
    reals, imags = four_point(reals, imags, 1.0)
    for j in range(1, 4):
        reals[j], imags[j] = turned(reals[j], imags[j], phase(tw_ref, 0, j), phase(tw_ref, 1, j))
    real, imag = jnp.concatenate(reals, axis=1), jnp.concatenate(imags, axis=1)
    lane = lax.broadcasted_iota(jnp.int32, (rows, SCALE_LANES), 1)
    tail = jnp.zeros((rows, SCALE_LANES), jnp.float32)
    for i in range(FOLD):
        own = slice(i * rows, (i + 1) * rows)
        conv = left_product(back_ref, jnp.concatenate([real[own], imag[own]], axis=0))
        exponent = wire_scale(conv)
        out_ref[:, i * span : (i + 1) * span] = conv * jnp.exp2(exponent)
        tail = jnp.where(lane == i, exponent, tail)
    out_ref[:, FOLD * span :] = tail


def mix_kernel(conv_ref, query_ref, key_ref, value_ref, gain_ref, out_ref, fold_ref):
    conv = load_folded(conv_ref, fold_ref, 1, 0).T
    driven = key_ref[...].astype(jnp.float32) * value_ref[...].astype(jnp.float32)
    mixed = query_ref[...].astype(jnp.float32) * (conv + gain_ref[...] * driven)
    out_ref[...] = mixed.astype(jnp.bfloat16)


def call(kernel, shape, dtype, name, vmem_mib, **more):
    return pl.pallas_call(
        kernel,
        out_shape=jax.ShapeDtypeStruct(shape, dtype),
        compiler_params=pltpu.CompilerParams(vmem_limit_bytes=vmem_mib * 2**20),
        name=name,
        **more,
    )


def on_wire(rows, shards):
    wide = rows.astype(jnp.float16).reshape(shards, rows.shape[0] // shards, rows.shape[1])
    return lax.optimization_barrier(regrouped(wide).reshape(rows.shape)).astype(jnp.float32)


def on_device(query, key_proj, value_proj, filter_taps, skip_gain):
    span, width = query.shape
    shards = lax.axis_size("seq")
    group = width // shards
    rows = width // FOLD
    folded = pltpu.VMEM((span // 128 + 1, width, 128), jnp.float32)
    unfolded = pltpu.VMEM((span // 128, width, 128), jnp.float32)
    phases = tables(shards, group, span)
    sources = [
        pltpu.with_memory_space_constraint(jnp.asarray(a), pltpu.HBM)
        for a in (key_proj, value_proj, filter_taps) + phases
    ]
    wire = jax.ShapeDtypeStruct((rows, 2 * FOLD * span + SCALE_LANES), jnp.float32)
    packed, *phases = pl.pallas_call(
        pack_kernel,
        out_shape=[wire] + [jax.ShapeDtypeStruct(a.shape, a.dtype) for a in phases],
        in_specs=[pl.BlockSpec(memory_space=pltpu.HBM)] * len(sources),
        out_specs=[pl.BlockSpec(memory_space=pltpu.VMEM)] * (1 + len(phases)),
        scratch_shapes=[
            pltpu.VMEM((span, width), jnp.bfloat16),
            pltpu.VMEM((span, width), jnp.bfloat16),
            pltpu.VMEM((span, width), jnp.float32),
            folded,
            pltpu.SemaphoreType.DMA((len(sources),)),
        ],
        compiler_params=pltpu.CompilerParams(vmem_limit_bytes=16 * 2**20),
        name="pack",
    )(*sources)
    conv = call(
        convolve_kernel,
        (rows, FOLD * span + SCALE_LANES),
        jnp.float32,
        "convolve",
        28,
    )(on_wire(packed, shards), *phases)
    mixed = call(mix_kernel, (span, width), jnp.bfloat16, "mix", 12, scratch_shapes=[unfolded])(
        on_wire(conv, shards), query, key_proj, value_proj, skip_gain[None, :]
    )
    return passed_along(mixed, "section", 1)


def solution(mesh):
    placed = (
        P("seq", "section"),
        P("seq", "section"),
        P("seq", "section"),
        P("seq", "section"),
        P("section"),
    )
    return jax.shard_map(
        on_device, mesh=mesh, in_specs=placed, out_specs=P("seq", "section"), check_vma=False
    )
```

```python
import jax
import jax.numpy as jnp
import numpy as np
from jax import lax
from jax.experimental import pallas as pl
from jax.experimental.pallas import tpu as pltpu
from jax.sharding import PartitionSpec as P

F16_TOP = 14.0
SCALE_LANES = 128
FOLD = 4
LAG_NANOS = 3300


def passed_along(value, axis, by):
    length = lax.axis_size(axis)
    return lax.ppermute(value, axis, [(i, (i + by) % length) for i in range(length)])


def regrouped(blocks):
    return lax.all_to_all(blocks, "seq", split_axis=0, concat_axis=0, tiled=True)


def split_bf16(table):
    high = table.astype(jnp.bfloat16)
    return high, (table - high.astype(np.float64)).astype(jnp.bfloat16)


def tables(shards, group, tok_rows):
    total = shards * tok_rows
    lanes = 128
    tiles = tok_rows // lanes
    s = np.arange(shards)
    k = np.arange(shards) + 0.25
    own = np.eye(group // FOLD)
    fwd_rows = []
    for j in range(tiles):
        turn = 2.0 * np.pi * np.outer(k, tiles * s + j) / (shards * tiles)
        fwd_rows.append(np.concatenate([np.kron(np.cos(turn), own), np.kron(-np.sin(turn), own)], axis=0))
    fwd_rows = np.stack(fwd_rows)
    turn = 2.0 * np.pi * np.outer(k, s) / shards
    inv_rows = np.concatenate([np.kron(np.cos(turn), own).T, np.kron(-np.sin(turn), own).T], axis=1) / total
    b = np.arange(lanes)
    turn = 2.0 * np.pi * np.outer(b, b) / lanes
    c, n = np.cos(turn), np.sin(turn)
    fwd_lanes = np.block([[c, -n], [n, c]])
    inv_lanes = np.block([[c, n], [-n, c]])
    near = np.repeat(2.0 * np.pi * np.outer(k, np.arange(tiles)) / (shards * tiles), lanes, axis=1)
    freq = k[:, None] + shards * np.repeat(np.arange(tiles), lanes)[None, :]
    far = 2.0 * np.pi * freq * np.tile(b, tiles)[None, :] / total
    twiddles = np.repeat(np.stack([np.cos(near), np.sin(near), np.cos(far), np.sin(far)]), group // FOLD, axis=1)
    rows_high, rows_low = split_bf16(fwd_rows)
    back_high, back_low = split_bf16(inv_rows)
    lane_high, lane_low = split_bf16(fwd_lanes)
    home_high, home_low = split_bf16(inv_lanes)
    return (
        np.concatenate([rows_high, rows_high, rows_low], axis=2),
        np.concatenate([back_high, back_high, back_low], axis=1),
        np.concatenate([lane_high, lane_low], axis=0),
        np.concatenate([home_high, home_low], axis=0),
        twiddles.astype(np.float32),
    )


def halves(value):
    high = value.astype(jnp.bfloat16)
    low = (value - high.astype(jnp.float32)).astype(jnp.bfloat16)
    return high, low


def left_product(table, value):
    high, low = halves(value)
    return jnp.dot(table, jnp.concatenate([high, low, high], axis=0), preferred_element_type=jnp.float32)


def right_product(value, table_ref):
    high, low = halves(value)
    depth = value.shape[1]
    table = jnp.concatenate([table_ref[:depth], table_ref[:depth], table_ref[depth:]], axis=0)
    return jnp.dot(jnp.concatenate([high, low, high], axis=1), table, preferred_element_type=jnp.float32)


def tile_of(value, index):
    return value[:, index * 128 : (index + 1) * 128]


def turned(real, imag, cosine, sine):
    return real * cosine - imag * sine, real * sine + imag * cosine


def four_point(r, q, sign):
    r02, q02, r13, q13 = r[0] + r[2], q[0] + q[2], r[1] + r[3], q[1] + q[3]
    d02, e02, d13, e13 = r[0] - r[2], q[0] - q[2], r[1] - r[3], q[1] - q[3]
    reals = [r02 + r13, d02 - sign * e13, r02 - r13, d02 + sign * e13]
    imags = [q02 + q13, e02 + sign * d13, q02 - q13, e02 - sign * d13]
    return reals, imags


def phase(tw_ref, part, tile):
    return tw_ref[part, :, tile * 128 : (tile + 1) * 128]


def wire_scale(rows):
    top = jnp.maximum(jnp.max(jnp.abs(rows), axis=1, keepdims=True), 1e-30)
    return F16_TOP - jnp.ceil(jnp.log2(top))


def store_folded(out_ref, fold_ref, parts):
    rows = out_ref.shape[0]
    span = parts[0].shape[1]
    lane = lax.broadcasted_iota(jnp.int32, (rows, SCALE_LANES), 1)
    tail = jnp.zeros((rows, SCALE_LANES), jnp.float32)
    for n, part in enumerate(parts):
        exponent = wire_scale(part)
        scaled = part * jnp.exp2(exponent)
        tiles = span // 128
        for tile in range(tiles):
            fold_ref[tile] = tile_of(scaled, tile)
        fold_ref[tiles] = jnp.broadcast_to(exponent, (part.shape[0], SCALE_LANES))
        for i in range(FOLD):
            at = (i * len(parts) + n) * span
            for tile in range(tiles):
                out_ref[:, at + tile * 128 : at + tile * 128 + 128] = fold_ref[tile, pl.ds(i, rows, stride=FOLD), :]
            own = fold_ref[tiles, pl.ds(i, rows, stride=FOLD), :]
            tail = jnp.where(lane == i * len(parts) + n, own, tail)
    out_ref[:, FOLD * len(parts) * span :] = tail


def load_folded(in_ref, fold_ref, count, n):
    rows, tiles = in_ref.shape[0], fold_ref.shape[0]
    for i in range(FOLD):
        lane = FOLD * count * tiles * 128 + i * count + n
        scale = jnp.exp2(-in_ref[:, lane : lane + 1])
        for tile in range(tiles):
            at = ((i * count + n) * tiles + tile) * 128
            fold_ref[tile, pl.ds(i, rows, stride=FOLD), :] = in_ref[:, at : at + 128] * scale
    return jnp.concatenate([fold_ref[tile] for tile in range(tiles)], axis=1)


def pack_kernel(*refs):
    count = (len(refs) - 8) // 2
    sources, outs = refs[: 3 + count], refs[3 + count : 4 + 2 * count]
    key_ref, value_ref, taps_ref, fold_ref, sems = refs[4 + 2 * count :]
    targets = (key_ref, value_ref, taps_ref) + outs[1:]
    copies = [pltpu.make_async_copy(a, b, sems.at[n]) for n, (a, b) in enumerate(zip(sources, targets))]
    for copy in copies:
        copy.start()
    copies[0].wait()
    copies[1].wait()
    driven = key_ref[...].astype(jnp.float32) * value_ref[...].astype(jnp.float32)
    copies[2].wait()

    @pl.when(lax.axis_index("section") % 2 == 0)
    def _():
        pl.delay(LAG_NANOS)

    store_folded(outs[0], fold_ref, [driven.T, taps_ref[...].T])
    for copy in copies[3:]:
        copy.wait()


def convolve_kernel(in_ref, rows_ref, back_ref, lanes_ref, home_ref, tw_ref, out_ref):
    rows, span = in_ref.shape[0], tw_ref.shape[2]

    def part(i, n):
        at, lane = (2 * i + n) * span, 2 * FOLD * span + 2 * i + n
        return in_ref[:, at : at + span] * jnp.exp2(-in_ref[:, lane : lane + 1])

    lane = lax.broadcasted_iota(jnp.int32, (rows, SCALE_LANES), 1)
    tail = jnp.zeros((rows, SCALE_LANES), jnp.float32)
    exponents, held = [None] * FOLD, [None] * FOLD

    def rows_step(i):
        sig, tap = part(i, 0), part(i, 1)
        outs = []
        for j in range(4):
            both = jnp.concatenate([tile_of(sig, j), tile_of(tap, j)], axis=1)
            outs.append(left_product(rows_ref[j], both))
        held[i] = outs

    def lanes_step(i):
        reals, imags = four_point([out[:rows] for out in held[i]], [out[rows:] for out in held[i]], -1.0)
        blocks = []
        for n in range(2):
            for m in range(4):
                cosine, sine = phase(tw_ref, 2, m), phase(tw_ref, 3, m)
                real, imag = turned(tile_of(reals[m], n), tile_of(imags[m], n), cosine, -sine)
                blocks.append(jnp.concatenate([real, imag], axis=1))
        held[i] = right_product(jnp.concatenate(blocks, axis=0), lanes_ref)

    def product_step(i):
        sig, tap = held[i][: 4 * rows], held[i][4 * rows :]
        product = turned(sig[:, :128], sig[:, 128:], tap[:, :128], tap[:, 128:])
        held[i] = right_product(jnp.concatenate(product, axis=1), home_ref)

    def back_step(i):
        reals, imags = [], []
        for m in range(4):
            own = held[i][m * rows : (m + 1) * rows]
            real, imag = turned(own[:, :128], own[:, 128:], phase(tw_ref, 2, m), phase(tw_ref, 3, m))
            reals.append(real)
            imags.append(imag)
        reals, imags = four_point(reals, imags, 1.0)
        for j in range(1, 4):
            reals[j], imags[j] = turned(reals[j], imags[j], phase(tw_ref, 0, j), phase(tw_ref, 1, j))
        parts = [jnp.concatenate(reals, axis=1), jnp.concatenate(imags, axis=1)]
        conv = left_product(back_ref[...], jnp.concatenate(parts, axis=0))
        exponents[i] = wire_scale(conv)
        out_ref[:, i * span : (i + 1) * span] = conv * jnp.exp2(exponents[i])

    steps = (rows_step, lanes_step, product_step, back_step)
    for step, i in ((0, 0), (0, 1), (1, 0), (0, 2), (1, 1), (2, 0), (0, 3), (1, 2), (2, 1), (3, 0), (1, 3), (2, 2), (3, 1), (2, 3), (3, 2), (3, 3)):
        steps[step](i)
    for i in range(FOLD):
        tail = jnp.where(lane == i, exponents[i], tail)
    out_ref[:, FOLD * span :] = tail


def mix_kernel(conv_ref, query_ref, key_ref, value_ref, gain_ref, out_ref, fold_ref):
    conv = load_folded(conv_ref, fold_ref, 1, 0).T
    driven = key_ref[...].astype(jnp.float32) * value_ref[...].astype(jnp.float32)
    mixed = query_ref[...].astype(jnp.float32) * (conv + gain_ref[...] * driven)
    out_ref[...] = mixed.astype(jnp.bfloat16)


def call(kernel, shape, dtype, name, vmem_mib, **more):
    return pl.pallas_call(
        kernel,
        out_shape=jax.ShapeDtypeStruct(shape, dtype),
        compiler_params=pltpu.CompilerParams(vmem_limit_bytes=vmem_mib * 2**20),
        name=name,
        **more,
    )


def on_wire(rows, shards):
    wide = rows.astype(jnp.float16).reshape(shards, rows.shape[0] // shards, rows.shape[1])
    return lax.optimization_barrier(regrouped(wide).reshape(rows.shape)).astype(jnp.float32)


def on_device(query, key_proj, value_proj, filter_taps, skip_gain):
    span, width = query.shape
    shards = lax.axis_size("seq")
    group = width // shards
    rows = width // FOLD
    folded = pltpu.VMEM((span // 128 + 1, width, 128), jnp.float32)
    unfolded = pltpu.VMEM((span // 128, width, 128), jnp.float32)
    phases = tables(shards, group, span)
    sources = [
        pltpu.with_memory_space_constraint(jnp.asarray(a), pltpu.HBM)
        for a in (key_proj, value_proj, filter_taps) + phases
    ]
    wire = jax.ShapeDtypeStruct((rows, 2 * FOLD * span + SCALE_LANES), jnp.float32)
    packed, *phases = pl.pallas_call(
        pack_kernel,
        out_shape=[wire] + [jax.ShapeDtypeStruct(a.shape, a.dtype) for a in phases],
        in_specs=[pl.BlockSpec(memory_space=pltpu.HBM)] * len(sources),
        out_specs=[pl.BlockSpec(memory_space=pltpu.VMEM)] * (1 + len(phases)),
        scratch_shapes=[
            pltpu.VMEM((span, width), jnp.bfloat16),
            pltpu.VMEM((span, width), jnp.bfloat16),
            pltpu.VMEM((span, width), jnp.float32),
            folded,
            pltpu.SemaphoreType.DMA((len(sources),)),
        ],
        compiler_params=pltpu.CompilerParams(vmem_limit_bytes=16 * 2**20),
        name="pack",
    )(*sources)
    conv = call(
        convolve_kernel,
        (rows, FOLD * span + SCALE_LANES),
        jnp.float32,
        "convolve",
        28,
    )(on_wire(packed, shards), *phases)
    mixed = call(mix_kernel, (span, width), jnp.bfloat16, "mix", 12, scratch_shapes=[unfolded])(
        on_wire(conv, shards), query, key_proj, value_proj, skip_gain[None, :]
    )
    return passed_along(mixed, "section", 1)


def solution(mesh):
    placed = (
        P("seq", "section"),
        P("seq", "section"),
        P("seq", "section"),
        P("seq", "section"),
        P("section"),
    )
    return jax.shard_map(
        on_device, mesh=mesh, in_specs=placed, out_specs=P("seq", "section"), check_vma=False
    )
```

```python
import jax
import jax.numpy as jnp
import numpy as np
from jax import lax
from jax.experimental import pallas as pl
from jax.experimental.pallas import tpu as pltpu
from jax.sharding import PartitionSpec as P

F16_TOP = 14.0
SCALE_LANES = 128
FOLD = 4
LAG_NANOS = 3300


def passed_along(value, axis, by):
    length = lax.axis_size(axis)
    return lax.ppermute(value, axis, [(i, (i + by) % length) for i in range(length)])


def regrouped(blocks):
    return lax.all_to_all(blocks, "seq", split_axis=0, concat_axis=0, tiled=True)


def split_bf16(table):
    high = table.astype(jnp.bfloat16)
    return high, (table - high.astype(np.float64)).astype(jnp.bfloat16)


def tables(shards, group, tok_rows):
    total = shards * tok_rows
    lanes = 128
    tiles = tok_rows // lanes
    s = np.arange(shards)
    k = np.arange(shards) + 0.25
    own = np.eye(group // FOLD)
    fwd_rows = []
    for j in range(tiles):
        turn = 2.0 * np.pi * np.outer(k, tiles * s + j) / (shards * tiles)
        fwd_rows.append(np.concatenate([np.kron(np.cos(turn), own), np.kron(-np.sin(turn), own)], axis=0))
    fwd_rows = np.stack(fwd_rows)
    turn = 2.0 * np.pi * np.outer(k, s) / shards
    inv_rows = np.concatenate([np.kron(np.cos(turn), own).T, np.kron(-np.sin(turn), own).T], axis=1) / total
    b = np.arange(lanes)
    turn = 2.0 * np.pi * np.outer(b, b) / lanes
    c, n = np.cos(turn), np.sin(turn)
    fwd_lanes = np.block([[c, -n], [n, c]])
    inv_lanes = np.block([[c, n], [-n, c]])
    near = np.repeat(2.0 * np.pi * np.outer(k, np.arange(tiles)) / (shards * tiles), lanes, axis=1)
    freq = k[:, None] + shards * np.repeat(np.arange(tiles), lanes)[None, :]
    far = 2.0 * np.pi * freq * np.tile(b, tiles)[None, :] / total
    twiddles = np.repeat(np.stack([np.cos(near), np.sin(near), np.cos(far), np.sin(far)]), group // FOLD, axis=1)
    rows_high, rows_low = split_bf16(fwd_rows)
    back_high, back_low = split_bf16(inv_rows)
    lane_high, lane_low = split_bf16(fwd_lanes)
    home_high, home_low = split_bf16(inv_lanes)
    return (
        np.concatenate([rows_high, rows_high, rows_low], axis=2),
        np.concatenate([back_high, back_high, back_low], axis=1),
        np.concatenate([lane_high, lane_low], axis=0),
        np.concatenate([home_high, home_low], axis=0),
        twiddles.astype(np.float32),
    )


def halves(value):
    high = value.astype(jnp.bfloat16)
    low = (value - high.astype(jnp.float32)).astype(jnp.bfloat16)
    return high, low


def left_product(table, value):
    high, low = halves(value)
    return jnp.dot(table, jnp.concatenate([high, low, high], axis=0), preferred_element_type=jnp.float32)


def right_product(value, table_ref):
    high, low = halves(value)
    depth = value.shape[1]
    table = jnp.concatenate([table_ref[:depth], table_ref[:depth], table_ref[depth:]], axis=0)
    return jnp.dot(jnp.concatenate([high, low, high], axis=1), table, preferred_element_type=jnp.float32)


def tile_of(value, index):
    return value[:, index * 128 : (index + 1) * 128]


def turned(real, imag, cosine, sine):
    return real * cosine - imag * sine, real * sine + imag * cosine


def four_point(r, q, sign):
    r02, q02, r13, q13 = r[0] + r[2], q[0] + q[2], r[1] + r[3], q[1] + q[3]
    d02, e02, d13, e13 = r[0] - r[2], q[0] - q[2], r[1] - r[3], q[1] - q[3]
    reals = [r02 + r13, d02 - sign * e13, r02 - r13, d02 + sign * e13]
    imags = [q02 + q13, e02 + sign * d13, q02 - q13, e02 - sign * d13]
    return reals, imags


def phase(tw_ref, part, tile):
    return tw_ref[part, :, tile * 128 : (tile + 1) * 128]


def wire_scale(rows):
    top = jnp.maximum(jnp.max(jnp.abs(rows), axis=1, keepdims=True), 1e-30)
    return F16_TOP - jnp.ceil(jnp.log2(top))


def store_folded(out_ref, fold_ref, parts):
    rows = out_ref.shape[0]
    span = (fold_ref.shape[0] - 1) * 128
    lane = lax.broadcasted_iota(jnp.int32, (rows, SCALE_LANES), 1)
    tail = jnp.zeros((rows, SCALE_LANES), jnp.float32)
    for n, take in enumerate(parts):
        part = take()
        exponent = wire_scale(part)
        scaled = part * jnp.exp2(exponent)
        tiles = span // 128
        for tile in range(tiles):
            fold_ref[tile] = tile_of(scaled, tile)
        fold_ref[tiles] = jnp.broadcast_to(exponent, (part.shape[0], SCALE_LANES))
        for i in range(FOLD):
            at = (i * len(parts) + n) * span
            for tile in range(tiles):
                out_ref[:, at + tile * 128 : at + tile * 128 + 128] = fold_ref[tile, pl.ds(i, rows, stride=FOLD), :]
            own = fold_ref[tiles, pl.ds(i, rows, stride=FOLD), :]
            tail = jnp.where(lane == i * len(parts) + n, own, tail)
    out_ref[:, FOLD * len(parts) * span :] = tail


def load_folded(in_ref, fold_ref, count, n):
    rows, tiles = in_ref.shape[0], fold_ref.shape[0]
    for i in range(FOLD):
        lane = FOLD * count * tiles * 128 + i * count + n
        scale = jnp.exp2(-in_ref[:, lane : lane + 1])
        for tile in range(tiles):
            at = ((i * count + n) * tiles + tile) * 128
            fold_ref[tile, pl.ds(i, rows, stride=FOLD), :] = in_ref[:, at : at + 128] * scale
    return jnp.concatenate([fold_ref[tile] for tile in range(tiles)], axis=1)


def pack_kernel(*refs):
    count = (len(refs) - 8) // 2
    sources, outs = refs[: 3 + count], refs[3 + count : 4 + 2 * count]
    key_ref, value_ref, taps_ref, fold_ref, sems = refs[4 + 2 * count :]
    targets = (key_ref, value_ref, taps_ref) + outs[1:]
    copies = [pltpu.make_async_copy(a, b, sems.at[n]) for n, (a, b) in enumerate(zip(sources, targets))]
    for copy in copies:
        copy.start()

    def signal():
        copies[0].wait()
        copies[1].wait()
        return (key_ref[...].astype(jnp.float32) * value_ref[...].astype(jnp.float32)).T

    def taps():
        copies[2].wait()
        return taps_ref[...].T

    store_folded(outs[0], fold_ref, [signal, taps])

    @pl.when(lax.axis_index("section") % 2 == 0)
    def _():
        pl.delay(LAG_NANOS)

    for copy in copies[3:]:
        copy.wait()


def convolve_kernel(in_ref, rows_ref, back_ref, lanes_ref, home_ref, tw_ref, out_ref):
    rows, span = in_ref.shape[0], tw_ref.shape[2]

    def part(i, n):
        at, lane = (2 * i + n) * span, 2 * FOLD * span + 2 * i + n
        return in_ref[:, at : at + span] * jnp.exp2(-in_ref[:, lane : lane + 1])

    lane = lax.broadcasted_iota(jnp.int32, (rows, SCALE_LANES), 1)
    tail = jnp.zeros((rows, SCALE_LANES), jnp.float32)
    exponents, held = [None] * FOLD, [None] * FOLD

    def rows_step(i):
        sig, tap = part(i, 0), part(i, 1)
        outs = []
        for j in range(4):
            both = jnp.concatenate([tile_of(sig, j), tile_of(tap, j)], axis=1)
            outs.append(left_product(rows_ref[j], both))
        held[i] = outs

    def lanes_step(i):
        reals, imags = four_point([out[:rows] for out in held[i]], [out[rows:] for out in held[i]], -1.0)
        blocks = []
        for n in range(2):
            for m in range(4):
                cosine, sine = phase(tw_ref, 2, m), phase(tw_ref, 3, m)
                real, imag = turned(tile_of(reals[m], n), tile_of(imags[m], n), cosine, -sine)
                blocks.append(jnp.concatenate([real, imag], axis=1))
        held[i] = right_product(jnp.concatenate(blocks, axis=0), lanes_ref)

    def product_step(i):
        sig, tap = held[i][: 4 * rows], held[i][4 * rows :]
        product = turned(sig[:, :128], sig[:, 128:], tap[:, :128], tap[:, 128:])
        held[i] = right_product(jnp.concatenate(product, axis=1), home_ref)

    def back_step(i):
        reals, imags = [], []
        for m in range(4):
            own = held[i][m * rows : (m + 1) * rows]
            real, imag = turned(own[:, :128], own[:, 128:], phase(tw_ref, 2, m), phase(tw_ref, 3, m))
            reals.append(real)
            imags.append(imag)
        reals, imags = four_point(reals, imags, 1.0)
        for j in range(1, 4):
            reals[j], imags[j] = turned(reals[j], imags[j], phase(tw_ref, 0, j), phase(tw_ref, 1, j))
        parts = [jnp.concatenate(reals, axis=1), jnp.concatenate(imags, axis=1)]
        conv = left_product(back_ref[...], jnp.concatenate(parts, axis=0))
        exponents[i] = wire_scale(conv)
        out_ref[:, i * span : (i + 1) * span] = conv * jnp.exp2(exponents[i])

    steps = (rows_step, lanes_step, product_step, back_step)
    for step, i in ((0, 0), (0, 1), (1, 0), (0, 2), (1, 1), (2, 0), (0, 3), (1, 2), (2, 1), (3, 0), (1, 3), (2, 2), (3, 1), (2, 3), (3, 2), (3, 3)):
        steps[step](i)
    for i in range(FOLD):
        tail = jnp.where(lane == i, exponents[i], tail)
    out_ref[:, FOLD * span :] = tail


def mix_kernel(conv_ref, query_ref, key_ref, value_ref, gain_ref, out_ref, fold_ref):
    conv = load_folded(conv_ref, fold_ref, 1, 0).T
    driven = key_ref[...].astype(jnp.float32) * value_ref[...].astype(jnp.float32)
    mixed = query_ref[...].astype(jnp.float32) * (conv + gain_ref[...] * driven)
    out_ref[...] = mixed.astype(jnp.bfloat16)


def call(kernel, shape, dtype, name, vmem_mib, **more):
    return pl.pallas_call(
        kernel,
        out_shape=jax.ShapeDtypeStruct(shape, dtype),
        compiler_params=pltpu.CompilerParams(vmem_limit_bytes=vmem_mib * 2**20),
        name=name,
        **more,
    )


def on_wire(rows, shards):
    wide = rows.astype(jnp.float16).reshape(shards, rows.shape[0] // shards, rows.shape[1])
    return lax.optimization_barrier(regrouped(wide).reshape(rows.shape)).astype(jnp.float32)


def on_device(query, key_proj, value_proj, filter_taps, skip_gain):
    span, width = query.shape
    shards = lax.axis_size("seq")
    group = width // shards
    rows = width // FOLD
    folded = pltpu.VMEM((span // 128 + 1, width, 128), jnp.float32)
    unfolded = pltpu.VMEM((span // 128, width, 128), jnp.float32)
    phases = tables(shards, group, span)
    sources = [
        pltpu.with_memory_space_constraint(jnp.asarray(a), pltpu.HBM)
        for a in (key_proj, value_proj, filter_taps) + phases
    ]
    wire = jax.ShapeDtypeStruct((rows, 2 * FOLD * span + SCALE_LANES), jnp.float32)
    packed, *phases = pl.pallas_call(
        pack_kernel,
        out_shape=[wire] + [jax.ShapeDtypeStruct(a.shape, a.dtype) for a in phases],
        in_specs=[pl.BlockSpec(memory_space=pltpu.HBM)] * len(sources),
        out_specs=[pl.BlockSpec(memory_space=pltpu.VMEM)] * (1 + len(phases)),
        scratch_shapes=[
            pltpu.VMEM((span, width), jnp.bfloat16),
            pltpu.VMEM((span, width), jnp.bfloat16),
            pltpu.VMEM((span, width), jnp.float32),
            folded,
            pltpu.SemaphoreType.DMA((len(sources),)),
        ],
        compiler_params=pltpu.CompilerParams(vmem_limit_bytes=16 * 2**20),
        name="pack",
    )(*sources)
    conv = call(
        convolve_kernel,
        (rows, FOLD * span + SCALE_LANES),
        jnp.float32,
        "convolve",
        28,
    )(on_wire(packed, shards), *phases)
    mixed = call(mix_kernel, (span, width), jnp.bfloat16, "mix", 12, scratch_shapes=[unfolded])(
        on_wire(conv, shards), query, key_proj, value_proj, skip_gain[None, :]
    )
    return passed_along(mixed, "section", 1)


def solution(mesh):
    placed = (
        P("seq", "section"),
        P("seq", "section"),
        P("seq", "section"),
        P("seq", "section"),
        P("section"),
    )
    return jax.shard_map(
        on_device, mesh=mesh, in_specs=placed, out_specs=P("seq", "section"), check_vma=False
    )
```
